32 devices in a mesh: obs: 4 (over y, x), par: 8 (over z, core).
Axes of the slice: x: 2, y: 2, z: 4, core: 2. Of those that a mesh axis runs over, the one named last changes fastest.
Arguments:
- jacobian: bfloat16 [2048, 32768], P('obs', 'par'), may hold values from -0.03125 to 0.03125
- probes: bfloat16 [32768, 256], P('par'), may hold values from -6 to 6
- coeffs: bfloat16 [256, 3, 128, 128], P('par'), may hold values from -0.3125 to 0.3125
- offsets: int32 [256, 2], P('par'), may hold values from -4 to 4
Outputs:
- ritz_basis: bfloat16 [32768, 256], P('par')
- basis_image: bfloat16 [32768, 256], P('par')
- ritz_matrix: float32 [256, 256], replicated
The draws below stay inside these ranges and needn't reach their ends.
All inputs are finite; a program needn't handle non-finite values.
Results may differ from the reference program's by a relative error of at most 0.015.
Values may be sent and summed in bfloat16 or wider, within the bound.
A program may use at most 128 MiB of HBM per device.

```python
import jax
import jax.numpy as jnp
from jax import lax

OBS_DEV = 512
K = 256
BLK = 128
REACH = 4
NOBS = 2048
NPAR = 32768
NBLK = 256
N_OBS = 4


def set_ends(values, rng, smallest, high):
    index_at = [jax.random.randint(jax.random.fold_in(rng, axis), (), 0, length) for axis, length in enumerate(values.shape)]
    longest = values.shape.index(max(values.shape))
    beside = index_at[:longest] + [(index_at[longest] + 1) % values.shape[longest]] + index_at[longest + 1:]
    return values.at[tuple(index_at)].set(smallest).at[tuple(beside)].set(high)


def block_levels(rng, shape, shards, smallest, high):
    gain, own = 1.0, jax.random.fold_in(rng, 6)
    for position, blocks in shards:
        steps = jnp.exp(jax.random.uniform(jax.random.fold_in(own, position), (blocks,), jnp.float32, smallest / len(shards), high / len(shards)))
        gain = gain * jnp.repeat(steps, shape[position] // blocks).reshape([-1 if axis == position else 1 for axis in range(len(shape))])
    return gain


def normal_values(key, extent, deviation, bound, split=(), held_as=jnp.bfloat16):
    entries = jax.random.normal(key, extent, jnp.float32) * deviation
    if len(split) > 0:
        entries = block_levels(key, extent, split, -0.22, 0.18) * entries
    return jnp.clip(entries, min=-bound, max=bound).astype(held_as)


def setup_inputs(seed: int = 0) -> dict:
    keys = jax.random.split(jax.random.key(seed), 5)
    jacobian = normal_values(keys[0], (NOBS, NPAR), NPAR ** -0.5, 0.03125, ((0, 4), (1, 8)))
    probes = normal_values(keys[1], (NPAR, K), 1.0, 6.0, ((0, 8),))
    coeffs = normal_values(keys[2], (NBLK, 3, BLK, BLK), (3 * BLK) ** -0.5, 0.3125, ((0, 8),))
    offsets = set_ends(jax.random.randint(keys[3], (NBLK, 2), -REACH, REACH + 1), jax.random.fold_in(keys[3], 1), -REACH, REACH).astype(jnp.int32)
    return dict(jacobian=jacobian, probes=probes, coeffs=coeffs, offsets=offsets)


def block_index(offsets):
    count = offsets.shape[0]
    full_offsets = jnp.concatenate([jnp.zeros((count, 1), jnp.int32), offsets.astype(jnp.int32)], axis=1)
    return (jnp.arange(count, dtype=jnp.int32)[:, None] + REACH + full_offsets).astype(jnp.int32)

def prior_forward(values, coeffs, offsets):
    width = values.shape[1]
    positions = block_index(offsets)
    padded = jnp.pad(values, ((REACH * BLK, REACH * BLK), (0, 0))).reshape(-1, BLK, width)
    picked = padded[positions]
    result = jnp.einsum('bjrc,bjcn->brn', coeffs.astype(jnp.float32), picked.astype(jnp.float32))
    return result.reshape(-1, width).astype(jnp.bfloat16)

def prior_adjoint(values, coeffs, offsets):
    width = values.shape[1]
    count = offsets.shape[0]
    positions = block_index(offsets)
    blocks = values.reshape(count, BLK, width)
    contrib = jnp.einsum('bjcr,bcn->bjrn', coeffs.astype(jnp.float32), blocks.astype(jnp.float32))
    accumulated = jnp.zeros((count + 2 * REACH, BLK, width), jnp.float32).at[positions].add(contrib)
    return accumulated[REACH:REACH + count].reshape(-1, width)

def reference(jacobian, probes, coeffs, offsets):
    sampled = prior_forward(probes, coeffs, offsets)
    forward = jnp.dot(jacobian.astype(jnp.float32), sampled.astype(jnp.float32), preferred_element_type=jnp.float32).astype(jnp.bfloat16)
    adjoint_total = jnp.zeros((NPAR, K), jnp.float32)
    for shard in range(N_OBS):
        jac_rows = jacobian[shard * OBS_DEV:(shard + 1) * OBS_DEV]
        fwd_rows = forward[shard * OBS_DEV:(shard + 1) * OBS_DEV]
        partial_sum = lax.dot_general(jac_rows.astype(jnp.float32), fwd_rows.astype(jnp.float32), (((0,), (0,)), ((), ())), preferred_element_type=jnp.float32)
        rounded = lax.optimization_barrier(partial_sum.astype(jnp.bfloat16))
        adjoint_total = adjoint_total + rounded.astype(jnp.float32)
    adjoint = adjoint_total.astype(jnp.bfloat16)
    range_sample = prior_adjoint(adjoint, coeffs, offsets)
    gram_matrix = jnp.dot(range_sample.T, range_sample, precision=lax.Precision.HIGHEST) / NPAR
    lower_factor = jnp.linalg.cholesky(gram_matrix)
    solved = lax.linalg.triangular_solve(lower_factor, range_sample, left_side=False, lower=True, transpose_a=True)
    ritz_basis = solved.astype(jnp.bfloat16)
    basis_image = prior_forward(ritz_basis, coeffs, offsets)
    projected = jnp.dot(jacobian.astype(jnp.float32), basis_image.astype(jnp.float32), preferred_element_type=jnp.float32)
    ritz_matrix = jnp.dot(projected.T, projected, precision=lax.Precision.HIGHEST) / NOBS
    return (ritz_basis, basis_image, ritz_matrix)
```

```python
import functools

import jax
import jax.numpy as jnp
from jax import lax
from jax.experimental import pallas as pl
from jax.experimental.pallas import tpu as pltpu
from jax.sharding import PartitionSpec as P

BLK = 128
REACH = 4
HALO = REACH * BLK
MESH = pl.DeviceIdType.MESH
F32 = jnp.float32
BF16 = jnp.bfloat16
VMEM = pl.BlockSpec(memory_space=pltpu.VMEM)
SMEM = pl.BlockSpec(memory_space=pltpu.SMEM)
LIMIT = 60 * 1024 * 1024


def greet(devices):
    barrier = pltpu.get_barrier_semaphore()
    for device in devices:
        pl.semaphore_signal(barrier, inc=1, device_id=device, device_id_type=MESH)
    pl.semaphore_wait(barrier, len(devices))


def remote(src, dst, send, recv, device):
    return pltpu.make_async_remote_copy(
        src_ref=src, dst_ref=dst, send_sem=send, recv_sem=recv, device_id=device, device_id_type=MESH
    )


def prior_block(b, base, source, coeffs, offs):
    def pick(offset):
        return source[b - base + offset]

    left = jnp.concatenate([coeffs[b, 0], coeffs[b, 1], coeffs[b, 2]], axis=1)
    right = jnp.concatenate([pick(0), pick(offs[b, 0]), pick(offs[b, 1])], axis=0)
    return jnp.dot(left, right, preferred_element_type=F32).astype(BF16)


def image_and_parts(n_par, o, p, offs, values, coeffs, jac, image, low, high, part, got, hs, hr, ps, pr):
    blocks = values.shape[0]
    side = 2 * REACH
    below = lax.rem(p + n_par - 1, n_par)
    above = lax.rem(p + 1, n_par)
    down = remote(values.at[pl.ds(0, REACH)], high.at[pl.ds(side, REACH)], hs.at[0], hr.at[0], (o, below))
    up = remote(values.at[pl.ds(blocks - REACH, REACH)], low.at[pl.ds(0, REACH)], hs.at[1], hr.at[1], (o, above))

    @pl.when(p > 0)
    def _():
        down.start()

    @pl.when(p < n_par - 1)
    def _():
        up.start()

    @pl.when(p == 0)
    def _():
        low[pl.ds(0, REACH)] = jnp.zeros((REACH,) + low.shape[1:], BF16)

    @pl.when(p == n_par - 1)
    def _():
        high[pl.ds(side, REACH)] = jnp.zeros((REACH,) + high.shape[1:], BF16)

    low[pl.ds(REACH, side)] = values[pl.ds(0, side)]
    high[pl.ds(0, side)] = values[pl.ds(blocks - side, side)]

    def inner(b, carry):
        image[pl.ds(pl.multiple_of(b * BLK, BLK), BLK), :] = prior_block(b, 0, values, coeffs, offs)
        return carry

    lax.fori_loop(REACH, blocks - REACH, inner, 0, unroll=4)

    @pl.when(p > 0)
    def _():
        down.wait_send()
        up.wait_recv()

    @pl.when(p < n_par - 1)
    def _():
        up.wait_send()
        down.wait_recv()

    for b in range(REACH):
        image[pl.ds(b * BLK, BLK), :] = prior_block(b, -REACH, low, coeffs, offs)
    for b in range(blocks - REACH, blocks):
        image[pl.ds(b * BLK, BLK), :] = prior_block(b, blocks - 2 * REACH, high, coeffs, offs)

    total = jnp.dot(jac[...], image[...], preferred_element_type=F32)
    piece = part.shape[1]
    for q in range(n_par):
        part[q] = total[q * piece : (q + 1) * piece].astype(BF16)
    copies = []
    for d in range(1, n_par):
        q = lax.rem(p + d, n_par)
        copy = remote(part.at[q], got.at[d], ps.at[d], pr.at[d], (o, q))
        copy.start()
        copies.append(copy)
    mine = part[p].astype(F32)
    for d in range(1, n_par):
        copies[d - 1].wait()
        mine = mine + got[d].astype(F32)
    return mine


def first_kernel(
    n_obs, n_par, offs, probes, coeffs, jac, out,
    image, low, high, part, got, fwd, adj, adj_got, hs, hr, ps, pr, gs, gr, os, orr,
):
    o, p = lax.axis_index("obs"), lax.axis_index("par")
    greet(
        [(o, lax.rem(p + d, n_par)) for d in range(1, n_par)]
        + [(lax.rem(o + d, n_obs), p) for d in range(1, n_obs)]
    )
    mine = image_and_parts(
        n_par, o, p, offs, probes, coeffs, jac, image, low, high, part, got, hs, hr, ps, pr
    )
    fwd[p] = mine.astype(BF16)
    copies = []
    for d in range(1, n_par):
        copy = remote(fwd.at[p], fwd.at[p], gs.at[d], gr.at[d], (o, lax.rem(p + d, n_par)))
        copy.start()
        copies.append(copy)
    for copy in copies:
        copy.wait()
    forward = fwd[...].reshape(jac.shape[0], fwd.shape[2])
    rows = adj.shape[1]
    tile = 256
    copies = []
    for d in list(range(1, n_obs)) + [0]:
        q = lax.rem(o + d, n_obs)

        def step(t, carry):
            start = pl.multiple_of(q * rows + t * tile, tile)
            value = lax.dot_general(
                jac[:, pl.ds(start, tile)], forward, (((0,), (0,)), ((), ())), preferred_element_type=F32
            )
            adj[d, pl.ds(pl.multiple_of(t * tile, tile), tile), :] = value.astype(BF16)
            return carry

        lax.fori_loop(0, rows // tile, step, 0)
        if d:
            copy = remote(adj.at[d], adj_got.at[d], os.at[d], orr.at[d], (q, p))
            copy.start()
            copies.append(copy)
    total = adj[0].astype(F32)
    for d in range(1, n_obs):
        copies[d - 1].wait()
        total = total + adj_got[d].astype(F32)
    out[...] = total.astype(BF16)


def adjoint_kernel(offs, values, coeffs, center, lower, upper, acc, held, sem):
    o = lax.axis_index("obs")
    blocks = values.shape[0] // BLK
    width = values.shape[1]
    load = pltpu.make_async_copy(coeffs.at[pl.ds(o * blocks, blocks)], held, sem.at[0])
    load.start()
    acc[...] = jnp.zeros_like(acc)
    load.wait()
    for b in range(blocks):
        v = values[pl.ds(b * BLK, BLK), :]
        for j in range(3):
            offset = 0 if j == 0 else offs[o * blocks + b, j - 1]
            where = pl.ds(pl.multiple_of((b + REACH + offset) * BLK, BLK), BLK)
            acc[where, :] += lax.dot_general(
                held[b, j], v, (((0,), (0,)), ((), ())), preferred_element_type=F32
            )
    lower[...] = acc[pl.ds(0, HALO), :].astype(BF16)
    center[...] = acc[pl.ds(HALO, blocks * BLK), :]
    upper[...] = acc[pl.ds(HALO + blocks * BLK, HALO), :].astype(BF16)


def everyone(n_obs, n_par, o, p):
    count = n_obs * n_par
    me = o * n_par + p
    others = []
    for d in range(1, count):
        k = lax.rem(me + d, count)
        others.append((k, (k // n_par, lax.rem(k, n_par))))
    return me, others


def sum_everywhere(me, others, value, send, got, out, ss, sr, gs, gr):
    count, piece, _ = send.shape
    for q in range(count):
        send[q] = value[q * piece : (q + 1) * piece]
    copies = []
    for d, (k, device) in enumerate(others, 1):
        copy = remote(send.at[k], got.at[d], ss.at[d], sr.at[d], device)
        copy.start()
        copies.append(copy)
    mine = send[me]
    for d, copy in enumerate(copies, 1):
        copy.wait()
        mine = mine + got[d]
    out[me] = mine
    copies = []
    for d, (k, device) in enumerate(others, 1):
        copy = remote(out.at[me], out.at[me], gs.at[d], gr.at[d], device)
        copy.start()
        copies.append(copy)
    return copies


def gram_kernel(
    n_obs, n_par, center, lower, upper, full, gram,
    sample, from_low, from_high, send, got, hs, hr, rs, rr, ss, sr, gs, gr,
):
    o, p = lax.axis_index("obs"), lax.axis_index("par")
    me, others = everyone(n_obs, n_par, o, p)
    greet([device for _, device in others])
    count = n_obs * n_par
    order = p * n_obs + o
    rows = center.shape[0]
    before = lax.rem(order + count - 1, count)
    after = lax.rem(order + 1, count)
    down = remote(lower, from_high, hs.at[0], hr.at[0], (lax.rem(before, n_obs), before // n_obs))
    up = remote(upper, from_low, hs.at[1], hr.at[1], (lax.rem(after, n_obs), after // n_obs))

    @pl.when(order > 0)
    def _():
        down.start()

    @pl.when(order < count - 1)
    def _():
        up.start()

    sample[...] = center[...]

    @pl.when(order > 0)
    def _():
        down.wait_send()
        up.wait_recv()
        sample[pl.ds(0, HALO), :] += from_low[...].astype(F32)

    @pl.when(order < count - 1)
    def _():
        up.wait_send()
        down.wait_recv()
        sample[pl.ds(rows - HALO, HALO), :] += from_high[...].astype(F32)

    full[o] = sample[...].astype(BF16)
    spread = []
    for d in range(1, n_obs):
        copy = remote(full.at[o], full.at[o], rs.at[d], rr.at[d], (lax.rem(o + d, n_obs), p))
        copy.start()
        spread.append(copy)
    value = lax.dot_general(
        sample[...], sample[...], (((0,), (0,)), ((), ())),
        precision=lax.Precision.HIGHEST, preferred_element_type=F32,
    ) / (rows * count)
    for copy in sum_everywhere(me, others, value, send, got, gram, ss, sr, gs, gr) + spread:
        copy.wait()


def second_kernel(
    n_obs, n_par, offs, basis, coeffs, jac, image, ritz,
    low, high, part, got, send, sum_got, hs, hr, ps, pr, ss, sr, gs, gr,
):
    o, p = lax.axis_index("obs"), lax.axis_index("par")
    me, others = everyone(n_obs, n_par, o, p)
    greet([device for _, device in others])
    mine = image_and_parts(
        n_par, o, p, offs, basis, coeffs, jac, image, low, high, part, got, hs, hr, ps, pr
    )
    value = lax.dot_general(
        mine, mine, (((0,), (0,)), ((), ())),
        precision=lax.Precision.HIGHEST, preferred_element_type=F32,
    ) / (jac.shape[0] * n_obs)
    for copy in sum_everywhere(me, others, value, send, sum_got, ritz, ss, sr, gs, gr):
        copy.wait()


def dma(count):
    return pltpu.SemaphoreType.DMA((count,))


def params(collective):
    return pltpu.CompilerParams(
        collective_id=collective, has_side_effects=True, vmem_limit_bytes=LIMIT
    )


def body(n_obs, n_par, jacobian, probes, coeffs, offsets):
    obs, rows = jacobian.shape
    width = probes.shape[1]
    own = rows // n_obs
    count = n_obs * n_par
    halos = [pltpu.VMEM((3 * REACH, BLK, width), BF16)] * 2
    parts = [pltpu.VMEM((n_par, obs // n_par, width), BF16)] * 2
    adjoint = pl.pallas_call(
        functools.partial(first_kernel, n_obs, n_par),
        out_shape=jax.ShapeDtypeStruct((own, width), BF16),
        in_specs=[SMEM, VMEM, VMEM, VMEM],
        out_specs=VMEM,
        scratch_shapes=[pltpu.VMEM((rows, width), BF16)]
        + halos
        + parts
        + [pltpu.VMEM((n_par, obs // n_par, width), BF16)]
        + [pltpu.VMEM((n_obs, own, width), BF16)] * 2
        + [dma(2)] * 2
        + [dma(n_par)] * 4
        + [dma(n_obs)] * 2,
        compiler_params=params(0),
        name="first_pass",
    )(offsets, probes.reshape(-1, BLK, width), coeffs, jacobian)
    center, lower, upper = pl.pallas_call(
        adjoint_kernel,
        out_shape=[
            jax.ShapeDtypeStruct((own, width), F32),
            jax.ShapeDtypeStruct((HALO, width), BF16),
            jax.ShapeDtypeStruct((HALO, width), BF16),
        ],
        in_specs=[SMEM, VMEM, pl.BlockSpec(memory_space=pl.ANY)],
        out_specs=[VMEM] * 3,
        scratch_shapes=[
            pltpu.VMEM((own + 2 * HALO, width), F32),
            pltpu.VMEM((own // BLK,) + coeffs.shape[1:], BF16),
            dma(1),
        ],
        compiler_params=pltpu.CompilerParams(vmem_limit_bytes=LIMIT),
        name="adjoint_prior",
    )(offsets, adjoint, coeffs)
    full, gram = pl.pallas_call(
        functools.partial(gram_kernel, n_obs, n_par),
        out_shape=[
            jax.ShapeDtypeStruct((n_obs, own, width), BF16),
            jax.ShapeDtypeStruct((count, width // count, width), F32),
        ],
        in_specs=[VMEM] * 3,
        out_specs=[VMEM] * 2,
        scratch_shapes=[pltpu.VMEM((own, width), F32)]
        + [pltpu.VMEM((HALO, width), BF16)] * 2
        + [pltpu.VMEM((count, width // count, width), F32)] * 2
        + [dma(2)] * 2
        + [dma(n_obs)] * 2
        + [dma(count)] * 4,
        compiler_params=params(1),
        name="gram",
    )(center, lower, upper)
    factor = jnp.linalg.cholesky(gram.reshape(width, width))
    inverse = lax.linalg.triangular_solve(
        factor, jnp.eye(width, dtype=F32), left_side=True, lower=True
    )
    high_part = inverse.astype(BF16)
    low_part = (inverse - high_part.astype(F32)).astype(BF16)
    sample = full.reshape(rows, width)
    last = (((1,), (1,)), ((), ()))
    basis = (
        lax.dot_general(sample, high_part, last, preferred_element_type=F32)
        + lax.dot_general(sample, low_part, last, preferred_element_type=F32)
    ).astype(BF16)
    image, ritz = pl.pallas_call(
        functools.partial(second_kernel, n_obs, n_par),
        out_shape=[
            jax.ShapeDtypeStruct((rows, width), BF16),
            jax.ShapeDtypeStruct((count, width // count, width), F32),
        ],
        in_specs=[SMEM, VMEM, VMEM, VMEM],
        out_specs=[VMEM] * 2,
        scratch_shapes=halos
        + parts
        + [pltpu.VMEM((count, width // count, width), F32)] * 2
        + [dma(2)] * 2
        + [dma(n_par)] * 2
        + [dma(count)] * 4,
        compiler_params=params(2),
        name="second_pass",
    )(offsets, basis.reshape(-1, BLK, width), coeffs, jacobian)
    return basis, image, ritz.reshape(width, width)


def solution(mesh):
    return jax.shard_map(
        functools.partial(body, mesh.shape["obs"], mesh.shape["par"]),
        mesh=mesh,
        in_specs=(P("obs", "par"), P("par", None), P("par", None, None, None), P("par", None)),
        out_specs=(P("par", None), P("par", None), P()),
        check_vma=False,
    )
```

```python
import functools

import jax
import jax.numpy as jnp
from jax import lax
from jax.experimental import pallas as pl
from jax.experimental.pallas import tpu as pltpu
from jax.sharding import PartitionSpec as P

BLK = 128
REACH = 4
HALO = REACH * BLK
MESH = pl.DeviceIdType.MESH
F32 = jnp.float32
BF16 = jnp.bfloat16
VMEM = pl.BlockSpec(memory_space=pltpu.VMEM)
SMEM = pl.BlockSpec(memory_space=pltpu.SMEM)
LIMIT = 60 * 1024 * 1024


def greet(devices):
    barrier = pltpu.get_barrier_semaphore()
    for device in devices:
        pl.semaphore_signal(barrier, inc=1, device_id=device, device_id_type=MESH)
    pl.semaphore_wait(barrier, len(devices))


def remote(src, dst, send, recv, device):
    return pltpu.make_async_remote_copy(
        src_ref=src, dst_ref=dst, send_sem=send, recv_sem=recv, device_id=device, device_id_type=MESH
    )


def prior_block(b, base, source, coeffs, offs):
    def pick(offset):
        return source[b - base + offset]

    left = jnp.concatenate([coeffs[b, 0], coeffs[b, 1], coeffs[b, 2]], axis=1)
    right = jnp.concatenate([pick(0), pick(offs[b, 0]), pick(offs[b, 1])], axis=0)
    return jnp.dot(left, right, preferred_element_type=F32).astype(BF16)


def image_and_parts(n_par, o, p, offs, values, coeffs, jac, image, low, high, part, got, hs, hr, ps, pr):
    blocks = values.shape[0]
    side = 2 * REACH
    below = lax.rem(p + n_par - 1, n_par)
    above = lax.rem(p + 1, n_par)
    down = remote(values.at[pl.ds(0, REACH)], high.at[pl.ds(side, REACH)], hs.at[0], hr.at[0], (o, below))
    up = remote(values.at[pl.ds(blocks - REACH, REACH)], low.at[pl.ds(0, REACH)], hs.at[1], hr.at[1], (o, above))

    @pl.when(p > 0)
    def _():
        down.start()

    @pl.when(p < n_par - 1)
    def _():
        up.start()

    @pl.when(p == 0)
    def _():
        low[pl.ds(0, REACH)] = jnp.zeros((REACH,) + low.shape[1:], BF16)

    @pl.when(p == n_par - 1)
    def _():
        high[pl.ds(side, REACH)] = jnp.zeros((REACH,) + high.shape[1:], BF16)

    low[pl.ds(REACH, side)] = values[pl.ds(0, side)]
    high[pl.ds(0, side)] = values[pl.ds(blocks - side, side)]

    def inner(b, carry):
        image[pl.ds(pl.multiple_of(b * BLK, BLK), BLK), :] = prior_block(b, 0, values, coeffs, offs)
        return carry

    lax.fori_loop(REACH, blocks - REACH, inner, 0, unroll=4)

    @pl.when(p > 0)
    def _():
        down.wait_send()
        up.wait_recv()

    @pl.when(p < n_par - 1)
    def _():
        up.wait_send()
        down.wait_recv()

    for b in range(REACH):
        image[pl.ds(b * BLK, BLK), :] = prior_block(b, -REACH, low, coeffs, offs)
    for b in range(blocks - REACH, blocks):
        image[pl.ds(b * BLK, BLK), :] = prior_block(b, blocks - 2 * REACH, high, coeffs, offs)

    total = jnp.dot(jac[...], image[...], preferred_element_type=F32)
    piece = part.shape[1]
    for q in range(n_par):
        part[q] = total[q * piece : (q + 1) * piece].astype(BF16)
    copies = []
    for d in range(1, n_par):
        q = lax.rem(p + d, n_par)
        copy = remote(part.at[q], got.at[d], ps.at[d], pr.at[d], (o, q))
        copy.start()
        copies.append(copy)
    mine = part[p].astype(F32)
    for d in range(1, n_par):
        copies[d - 1].wait()
        mine = mine + got[d].astype(F32)
    return mine


def first_kernel(
    n_obs, n_par, offs, probes, coeffs, jac, out,
    image, low, high, part, got, fwd, adj, adj_got, hs, hr, ps, pr, gs, gr, os, orr,
):
    o, p = lax.axis_index("obs"), lax.axis_index("par")
    greet(
        [(o, lax.rem(p + d, n_par)) for d in range(1, n_par)]
        + [(lax.rem(o + d, n_obs), p) for d in range(1, n_obs)]
    )
    mine = image_and_parts(
        n_par, o, p, offs, probes, coeffs, jac, image, low, high, part, got, hs, hr, ps, pr
    )
    fwd[p] = mine.astype(BF16)
    copies = []
    for d in range(1, n_par):
        copy = remote(fwd.at[p], fwd.at[p], gs.at[d], gr.at[d], (o, lax.rem(p + d, n_par)))
        copy.start()
        copies.append(copy)
    for copy in copies:
        copy.wait()
    forward = fwd[...].reshape(jac.shape[0], fwd.shape[2])
    rows = adj.shape[1]
    tile = 256
    copies = []
    for d in list(range(1, n_obs)) + [0]:
        q = lax.rem(o + d, n_obs)

        def step(t, carry):
            start = pl.multiple_of(q * rows + t * tile, tile)
            value = lax.dot_general(
                jac[:, pl.ds(start, tile)], forward, (((0,), (0,)), ((), ())), preferred_element_type=F32
            )
            adj[d, pl.ds(pl.multiple_of(t * tile, tile), tile), :] = value.astype(BF16)
            return carry

        lax.fori_loop(0, rows // tile, step, 0)
        if d:
            copy = remote(adj.at[d], adj_got.at[d], os.at[d], orr.at[d], (q, p))
            copy.start()
            copies.append(copy)
    total = adj[0].astype(F32)
    for d in range(1, n_obs):
        copies[d - 1].wait()
        total = total + adj_got[d].astype(F32)
    out[...] = total.astype(BF16)


def adjoint_kernel(offs, values, coeffs, center, lower, upper, acc, held, sem):
    o = lax.axis_index("obs")
    blocks = values.shape[0] // BLK
    width = values.shape[1]
    load = pltpu.make_async_copy(coeffs.at[pl.ds(o * blocks, blocks)], held, sem.at[0])
    load.start()
    acc[...] = jnp.zeros_like(acc)
    load.wait()
    for b in range(blocks):
        v = values[pl.ds(b * BLK, BLK), :]
        for j in range(3):
            offset = 0 if j == 0 else offs[o * blocks + b, j - 1]
            where = pl.ds(pl.multiple_of((b + REACH + offset) * BLK, BLK), BLK)
            acc[where, :] += lax.dot_general(
                held[b, j], v, (((0,), (0,)), ((), ())), preferred_element_type=F32
            )
    lower[...] = acc[pl.ds(0, HALO), :].astype(BF16)
    center[...] = acc[pl.ds(HALO, blocks * BLK), :]
    upper[...] = acc[pl.ds(HALO + blocks * BLK, HALO), :].astype(BF16)


def everyone(n_obs, n_par, o, p):
    count = n_obs * n_par
    me = o * n_par + p
    others = []
    for d in range(1, count):
        k = lax.rem(me + d, count)
        others.append((k, (k // n_par, lax.rem(k, n_par))))
    return me, others


def sum_everywhere(me, others, value, send, got, out, ss, sr, gs, gr):
    count, piece, _ = send.shape
    for q in range(count):
        send[q] = value[q * piece : (q + 1) * piece]
    copies = []
    for d, (k, device) in enumerate(others, 1):
        copy = remote(send.at[k], got.at[d], ss.at[d], sr.at[d], device)
        copy.start()
        copies.append(copy)
    mine = send[me]
    for d, copy in enumerate(copies, 1):
        copy.wait()
        mine = mine + got[d]
    out[me] = mine
    copies = []
    for d, (k, device) in enumerate(others, 1):
        copy = remote(out.at[me], out.at[me], gs.at[d], gr.at[d], device)
        copy.start()
        copies.append(copy)
    return copies


def small_inverse_factor(matrix):
    size = matrix.shape[0]
    row = lax.broadcasted_iota(jnp.int32, (size, size), 0)
    lane = lax.broadcasted_iota(jnp.int32, (size, size), 1)
    work = jnp.concatenate([matrix, (row == lane).astype(F32)], axis=1)
    group = 8
    parts = [work[g : g + group] for g in range(0, size, group)]
    index = lax.broadcasted_iota(jnp.int32, (group, 2 * size), 0)
    scales = []
    for j in range(size):
        first, at = j // group, j % group
        columns = [jnp.broadcast_to(part[:, j : j + 1], part.shape) for part in parts[first:]]
        pivot = columns[0][at : at + 1]
        scales.append(lax.rsqrt(pivot))
        scaled = parts[first][at : at + 1] * (1.0 / pivot)
        for g, column in enumerate(columns):
            if g == 0:
                column = jnp.where(index > at, column, 0.0)
            parts[first + g] = parts[first + g] - column * scaled
    rows = [parts[j // group][j % group : j % group + 1] * scales[j] for j in range(size)]
    return jnp.concatenate(rows, axis=0)[:, size:]


def inverse_factor(gram, work, out, size):
    blocks = work.shape[0]
    width = blocks * size
    row = lax.broadcasted_iota(jnp.int32, (size, width), 0)
    lane = lax.broadcasted_iota(jnp.int32, (size, width), 1)
    for k in range(blocks):
        work[k, :, pl.ds(0, width)] = gram[k * size : (k + 1) * size]
        work[k, :, pl.ds(width, width)] = (lane == row + k * size).astype(F32)

    def step(k, carry):
        rows = work[k]
        shift = lax.rem(width - k * size, width)
        diagonal = pltpu.roll(rows[:, :width], shift, 1)[:, :size]
        small = small_inverse_factor(diagonal)
        upper = jnp.dot(small, rows, precision=lax.Precision.HIGHEST, preferred_element_type=F32)
        out[k] = upper[:, width:]
        left = jnp.where(lane >= (k + 1) * size, upper[:, :width], 0.0)
        update = lax.dot_general(
            left, upper, (((0,), (0,)), ((), ())),
            precision=lax.Precision.HIGHEST, preferred_element_type=F32,
        )
        for i in range(blocks):
            work[i] -= update[i * size : (i + 1) * size]
        return carry

    lax.fori_loop(0, blocks, step, 0)


def gram_kernel(
    n_obs, n_par, center, lower, upper, full, inverse,
    sample, from_low, from_high, send, got, gram, work, hs, hr, rs, rr, ss, sr, gs, gr,
):
    o, p = lax.axis_index("obs"), lax.axis_index("par")
    me, others = everyone(n_obs, n_par, o, p)
    greet([device for _, device in others])
    count = n_obs * n_par
    order = p * n_obs + o
    rows = center.shape[0]
    before = lax.rem(order + count - 1, count)
    after = lax.rem(order + 1, count)
    down = remote(lower, from_high, hs.at[0], hr.at[0], (lax.rem(before, n_obs), before // n_obs))
    up = remote(upper, from_low, hs.at[1], hr.at[1], (lax.rem(after, n_obs), after // n_obs))

    @pl.when(order > 0)
    def _():
        down.start()

    @pl.when(order < count - 1)
    def _():
        up.start()

    sample[...] = center[...]

    @pl.when(order > 0)
    def _():
        down.wait_send()
        up.wait_recv()
        sample[pl.ds(0, HALO), :] += from_low[...].astype(F32)

    @pl.when(order < count - 1)
    def _():
        up.wait_send()
        down.wait_recv()
        sample[pl.ds(rows - HALO, HALO), :] += from_high[...].astype(F32)

    full[o] = sample[...].astype(BF16)
    value = lax.dot_general(
        sample[...], sample[...], (((0,), (0,)), ((), ())),
        precision=lax.Precision.HIGHEST, preferred_element_type=F32,
    ) / (rows * count)
    copies = sum_everywhere(me, others, value, send, got, gram, ss, sr, gs, gr)
    spread = []
    for d in range(1, n_obs):
        copy = remote(full.at[o], full.at[o], rs.at[d], rr.at[d], (lax.rem(o + d, n_obs), p))
        copy.start()
        spread.append(copy)
    for copy in copies:
        copy.wait()
    matrix = jnp.concatenate([gram[q] for q in range(count)], axis=0)
    inverse_factor(matrix, work, inverse, inverse.shape[1])
    for copy in spread:
        copy.wait()


def second_kernel(
    n_obs, n_par, offs, basis, coeffs, jac, image, ritz,
    low, high, part, got, send, sum_got, hs, hr, ps, pr, ss, sr, gs, gr,
):
    o, p = lax.axis_index("obs"), lax.axis_index("par")
    me, others = everyone(n_obs, n_par, o, p)
    greet([device for _, device in others])
    mine = image_and_parts(
        n_par, o, p, offs, basis, coeffs, jac, image, low, high, part, got, hs, hr, ps, pr
    )
    value = lax.dot_general(
        mine, mine, (((0,), (0,)), ((), ())),
        precision=lax.Precision.HIGHEST, preferred_element_type=F32,
    ) / (jac.shape[0] * n_obs)
    for copy in sum_everywhere(me, others, value, send, sum_got, ritz, ss, sr, gs, gr):
        copy.wait()


def dma(count):
    return pltpu.SemaphoreType.DMA((count,))


def params(collective):
    return pltpu.CompilerParams(
        collective_id=collective, has_side_effects=True, vmem_limit_bytes=LIMIT
    )


def body(n_obs, n_par, jacobian, probes, coeffs, offsets):
    obs, rows = jacobian.shape
    width = probes.shape[1]
    own = rows // n_obs
    count = n_obs * n_par
    halos = [pltpu.VMEM((3 * REACH, BLK, width), BF16)] * 2
    parts = [pltpu.VMEM((n_par, obs // n_par, width), BF16)] * 2
    adjoint = pl.pallas_call(
        functools.partial(first_kernel, n_obs, n_par),
        out_shape=jax.ShapeDtypeStruct((own, width), BF16),
        in_specs=[SMEM, VMEM, VMEM, VMEM],
        out_specs=VMEM,
        scratch_shapes=[pltpu.VMEM((rows, width), BF16)]
        + halos
        + parts
        + [pltpu.VMEM((n_par, obs // n_par, width), BF16)]
        + [pltpu.VMEM((n_obs, own, width), BF16)] * 2
        + [dma(2)] * 2
        + [dma(n_par)] * 4
        + [dma(n_obs)] * 2,
        compiler_params=params(0),
        name="first_pass",
    )(offsets, probes.reshape(-1, BLK, width), coeffs, jacobian)
    center, lower, upper = pl.pallas_call(
        adjoint_kernel,
        out_shape=[
            jax.ShapeDtypeStruct((own, width), F32),
            jax.ShapeDtypeStruct((HALO, width), BF16),
            jax.ShapeDtypeStruct((HALO, width), BF16),
        ],
        in_specs=[SMEM, VMEM, pl.BlockSpec(memory_space=pl.ANY)],
        out_specs=[VMEM] * 3,
        scratch_shapes=[
            pltpu.VMEM((own + 2 * HALO, width), F32),
            pltpu.VMEM((own // BLK,) + coeffs.shape[1:], BF16),
            dma(1),
        ],
        compiler_params=pltpu.CompilerParams(vmem_limit_bytes=LIMIT),
        name="adjoint_prior",
    )(offsets, adjoint, coeffs)
    block = 64
    full, inverse = pl.pallas_call(
        functools.partial(gram_kernel, n_obs, n_par),
        out_shape=[
            jax.ShapeDtypeStruct((n_obs, own, width), BF16),
            jax.ShapeDtypeStruct((width // block, block, width), F32),
        ],
        in_specs=[VMEM] * 3,
        out_specs=[VMEM] * 2,
        scratch_shapes=[pltpu.VMEM((own, width), F32)]
        + [pltpu.VMEM((HALO, width), BF16)] * 2
        + [pltpu.VMEM((count, width // count, width), F32)] * 3
        + [pltpu.VMEM((width // block, block, 2 * width), F32)]
        + [dma(2)] * 2
        + [dma(n_obs)] * 2
        + [dma(count)] * 4,
        compiler_params=params(1),
        name="gram",
    )(center, lower, upper)
    inverse = inverse.reshape(width, width)
    high_part = inverse.astype(BF16)
    low_part = (inverse - high_part.astype(F32)).astype(BF16)
    sample = full.reshape(rows, width)
    last = (((1,), (1,)), ((), ()))
    basis = (
        lax.dot_general(sample, high_part, last, preferred_element_type=F32)
        + lax.dot_general(sample, low_part, last, preferred_element_type=F32)
    ).astype(BF16)
    image, ritz = pl.pallas_call(
        functools.partial(second_kernel, n_obs, n_par),
        out_shape=[
            jax.ShapeDtypeStruct((rows, width), BF16),
            jax.ShapeDtypeStruct((count, width // count, width), F32),
        ],
        in_specs=[SMEM, VMEM, VMEM, VMEM],
        out_specs=[VMEM] * 2,
        scratch_shapes=halos
        + parts
        + [pltpu.VMEM((count, width // count, width), F32)] * 2
        + [dma(2)] * 2
        + [dma(n_par)] * 2
        + [dma(count)] * 4,
        compiler_params=params(2),
        name="second_pass",
    )(offsets, basis.reshape(-1, BLK, width), coeffs, jacobian)
    return basis, image, ritz.reshape(width, width)


def solution(mesh):
    return jax.shard_map(
        functools.partial(body, mesh.shape["obs"], mesh.shape["par"]),
        mesh=mesh,
        in_specs=(P("obs", "par"), P("par", None), P("par", None, None, None), P("par", None)),
        out_specs=(P("par", None), P("par", None), P()),
        check_vma=False,
    )
```

```python
import functools

import jax
import jax.numpy as jnp
from jax import lax
from jax.experimental import pallas as pl
from jax.experimental.pallas import tpu as pltpu
from jax.sharding import PartitionSpec as P

BLK = 128
REACH = 4
HALO = REACH * BLK
MESH = pl.DeviceIdType.MESH
F32 = jnp.float32
BF16 = jnp.bfloat16
VMEM = pl.BlockSpec(memory_space=pltpu.VMEM)
SMEM = pl.BlockSpec(memory_space=pltpu.SMEM)
LIMIT = 60 * 1024 * 1024


def greet(devices):
    barrier = pltpu.get_barrier_semaphore()
    for device in devices:
        pl.semaphore_signal(barrier, inc=1, device_id=device, device_id_type=MESH)
    pl.semaphore_wait(barrier, len(devices))


def remote(src, dst, send, recv, device):
    return pltpu.make_async_remote_copy(
        src_ref=src, dst_ref=dst, send_sem=send, recv_sem=recv, device_id=device, device_id_type=MESH
    )


def prior_block(b, base, source, coeffs, offs):
    def pick(offset):
        return source[b - base + offset]

    left = jnp.concatenate([coeffs[b, 0], coeffs[b, 1], coeffs[b, 2]], axis=1)
    right = jnp.concatenate([pick(0), pick(offs[b, 0]), pick(offs[b, 1])], axis=0)
    return jnp.dot(left, right, preferred_element_type=F32).astype(BF16)


def fetch(source, coeffs, jac, values, held, jac_held, low, high, sem):
    blocks = source.shape[0]
    side = 2 * REACH
    loads = [
        pltpu.make_async_copy(source, values, sem.at[0]),
        pltpu.make_async_copy(coeffs, held, sem.at[1]),
        pltpu.make_async_copy(source.at[pl.ds(0, side)], low.at[pl.ds(REACH, side)], sem.at[2]),
        pltpu.make_async_copy(source.at[pl.ds(blocks - side, side)], high.at[pl.ds(0, side)], sem.at[3]),
        pltpu.make_async_copy(jac, jac_held, sem.at[4]),
    ]
    for load in loads:
        load.start()
    return loads


def image_and_parts(
    n_par, o, p, offs, source, loads, values, coeffs, jac, image, low, high, part, got, hs, hr, ps, pr
):
    blocks = values.shape[0]
    side = 2 * REACH
    below = lax.rem(p + n_par - 1, n_par)
    above = lax.rem(p + 1, n_par)
    down = remote(source.at[pl.ds(0, REACH)], high.at[pl.ds(side, REACH)], hs.at[0], hr.at[0], (o, below))
    up = remote(source.at[pl.ds(blocks - REACH, REACH)], low.at[pl.ds(0, REACH)], hs.at[1], hr.at[1], (o, above))

    @pl.when(p > 0)
    def _():
        down.start()

    @pl.when(p < n_par - 1)
    def _():
        up.start()

    @pl.when(p == 0)
    def _():
        low[pl.ds(0, REACH)] = jnp.zeros((REACH,) + low.shape[1:], BF16)

    @pl.when(p == n_par - 1)
    def _():
        high[pl.ds(side, REACH)] = jnp.zeros((REACH,) + high.shape[1:], BF16)

    loads[0].wait()
    loads[1].wait()

    def inner(b, carry):
        image[pl.ds(pl.multiple_of(b * BLK, BLK), BLK), :] = prior_block(b, 0, values, coeffs, offs)
        return carry

    lax.fori_loop(REACH, blocks - REACH, inner, 0, unroll=4)

    @pl.when(p > 0)
    def _():
        down.wait_send()
        up.wait_recv()

    @pl.when(p < n_par - 1)
    def _():
        up.wait_send()
        down.wait_recv()

    loads[2].wait()
    loads[3].wait()
    for b in range(REACH):
        image[pl.ds(b * BLK, BLK), :] = prior_block(b, -REACH, low, coeffs, offs)
    for b in range(blocks - REACH, blocks):
        image[pl.ds(b * BLK, BLK), :] = prior_block(b, blocks - 2 * REACH, high, coeffs, offs)

    loads[4].wait()
    total = jnp.dot(jac[...], image[...], preferred_element_type=F32)
    piece = part.shape[1]
    for q in range(n_par):
        part[q] = total[q * piece : (q + 1) * piece].astype(BF16)
    copies = []
    for d in range(1, n_par):
        q = lax.rem(p + d, n_par)
        copy = remote(part.at[q], got.at[d], ps.at[d], pr.at[d], (o, q))
        copy.start()
        copies.append(copy)
    mine = part[p].astype(F32)
    for d in range(1, n_par):
        copies[d - 1].wait()
        mine = mine + got[d].astype(F32)
    return mine


def first_kernel(
    n_obs, n_par, offs, probes, coeffs, jac_ref, out,
    low, high, values, held, jac, ls, image, part, got, fwd, adj, adj_got, hs, hr, ps, pr, gs, gr, os, orr,
):
    o, p = lax.axis_index("obs"), lax.axis_index("par")
    loads = fetch(probes, coeffs, jac_ref, values, held, jac, low, high, ls)
    greet(
        [(o, lax.rem(p + d, n_par)) for d in range(1, n_par)]
        + [(lax.rem(o + d, n_obs), p) for d in range(1, n_obs)]
    )
    mine = image_and_parts(
        n_par, o, p, offs, probes, loads, values, held, jac, image, low, high,
        part, got, hs, hr, ps, pr,
    )
    fwd[p] = mine.astype(BF16)
    copies = []
    for d in range(1, n_par):
        copy = remote(fwd.at[p], fwd.at[p], gs.at[d], gr.at[d], (o, lax.rem(p + d, n_par)))
        copy.start()
        copies.append(copy)
    for copy in copies:
        copy.wait()
    forward = fwd[...].reshape(jac.shape[0], fwd.shape[2])
    rows = adj.shape[1]
    tile = 256
    copies = []
    for d in list(range(1, n_obs)) + [0]:
        q = lax.rem(o + d, n_obs)

        def step(t, carry):
            start = pl.multiple_of(q * rows + t * tile, tile)
            value = lax.dot_general(
                jac[:, pl.ds(start, tile)], forward, (((0,), (0,)), ((), ())), preferred_element_type=F32
            )
            adj[d, pl.ds(pl.multiple_of(t * tile, tile), tile), :] = value.astype(BF16)
            return carry

        lax.fori_loop(0, rows // tile, step, 0)
        if d:
            copy = remote(adj.at[d], adj_got.at[d], os.at[d], orr.at[d], (q, p))
            copy.start()
            copies.append(copy)
    total = adj[0].astype(F32)
    for d in range(1, n_obs):
        copies[d - 1].wait()
        total = total + adj_got[d].astype(F32)
    out[...] = total.astype(BF16)


def adjoint_kernel(offs, values, coeffs, center, lower, upper, acc, held, sem):
    o = lax.axis_index("obs")
    blocks = values.shape[0] // BLK
    width = values.shape[1]
    load = pltpu.make_async_copy(coeffs.at[pl.ds(o * blocks, blocks)], held, sem.at[0])
    load.start()
    acc[...] = jnp.zeros_like(acc)
    load.wait()
    for b in range(blocks):
        v = values[pl.ds(b * BLK, BLK), :]
        for j in range(3):
            offset = 0 if j == 0 else offs[o * blocks + b, j - 1]
            where = pl.ds(pl.multiple_of((b + REACH + offset) * BLK, BLK), BLK)
            acc[where, :] += lax.dot_general(
                held[b, j], v, (((0,), (0,)), ((), ())), preferred_element_type=F32
            )
    lower[...] = acc[pl.ds(0, HALO), :].astype(BF16)
    center[...] = acc[pl.ds(HALO, blocks * BLK), :]
    upper[...] = acc[pl.ds(HALO + blocks * BLK, HALO), :].astype(BF16)


def groups(n_obs, n_par, o, p):
    along_obs = [(lax.rem(o + d, n_obs), p) for d in range(1, n_obs)]
    along_par = [(o, lax.rem(p + d, n_par)) for d in range(1, n_par)]
    return along_obs, along_par


def swap(send, got, index, devices, send_sem, recv_sem):
    copies = []
    for d, device in enumerate(devices, 1):
        copy = remote(send.at[device[index]], got.at[d], send_sem.at[d], recv_sem.at[d], device)
        copy.start()
        copies.append(copy)
    return copies


def spread_out(ref, devices, send_sem, recv_sem):
    copies = []
    for d, device in enumerate(devices, 1):
        copy = remote(ref, ref, send_sem.at[d], recv_sem.at[d], device)
        copy.start()
        copies.append(copy)
    return copies


def sum_everywhere(o, p, devices, value, send1, got1, send2, got2, out, sems):
    along_obs, along_par = devices
    n_obs, n_par, piece, _ = out.shape
    kind = out.dtype
    tall = n_par * piece
    for q in range(n_obs):
        send1[q] = value[q * tall : (q + 1) * tall].astype(kind)
    copies = swap(send1, got1, 0, along_obs, sems[0], sems[1])
    mine = send1[o].astype(F32)
    for d, copy in enumerate(copies, 1):
        copy.wait()
        mine = mine + got1[d].astype(F32)
    for q in range(n_par):
        send2[q] = mine[q * piece : (q + 1) * piece].astype(kind)
    copies = swap(send2, got2, 1, along_par, sems[2], sems[3])
    mine = send2[p].astype(F32)
    for d, copy in enumerate(copies, 1):
        copy.wait()
        mine = mine + got2[d].astype(F32)
    out[o, p] = mine.astype(kind)
    for copy in spread_out(out.at[o, p], along_par, sems[4], sems[5]):
        copy.wait()
    for copy in spread_out(out.at[o], along_obs, sems[6], sems[7]):
        copy.wait()


def sum_scratch(n_obs, n_par, width, kind):
    tall = width // n_obs
    return (
        [pltpu.VMEM((n_obs, tall, width), kind)] * 2
        + [pltpu.VMEM((n_par, tall // n_par, width), kind)] * 2
        + [dma(n_obs)] * 2
        + [dma(n_par)] * 4
        + [dma(n_obs)] * 2
    )


def small_inverse_factor(matrix):
    size = matrix.shape[0]
    row = lax.broadcasted_iota(jnp.int32, (size, size), 0)
    lane = lax.broadcasted_iota(jnp.int32, (size, size), 1)
    work = jnp.concatenate([matrix, (row == lane).astype(F32)], axis=1)
    group = 8
    parts = [work[g : g + group] for g in range(0, size, group)]
    index = lax.broadcasted_iota(jnp.int32, (group, 2 * size), 0)
    scales = []
    for first in range(size // group):
        start = first * group
        columns = [
            [jnp.broadcast_to(part[:, start + t : start + t + 1], part.shape) for part in parts[first:]]
            for t in range(group)
        ]
        for t in range(group):
            pivot = columns[t][0][t : t + 1]
            scales.append(lax.rsqrt(pivot))
            reciprocal = 1.0 / pivot
            scaled = parts[first][t : t + 1] * reciprocal
            columns[t][0] = jnp.where(index > t, columns[t][0], 0.0)
            for u in range(t + 1, group):
                ratio = columns[u][0][t : t + 1] * reciprocal
                columns[u] = [c - e * ratio for c, e in zip(columns[u], columns[t])]
            for g, column in enumerate(columns[t]):
                parts[first + g] = parts[first + g] - column * scaled
    rows = [parts[j // group][j % group : j % group + 1] * scales[j] for j in range(size)]
    return jnp.concatenate(rows, axis=0)[:, size:]


def inverse_factor(gram, work, out, size):
    blocks = work.shape[0]
    width = blocks * size
    row = lax.broadcasted_iota(jnp.int32, (size, width), 0)
    lane = lax.broadcasted_iota(jnp.int32, (size, width), 1)
    for k in range(blocks):
        work[k, :, pl.ds(0, width)] = gram[k * size : (k + 1) * size]
        work[k, :, pl.ds(width, width)] = (lane == row + k * size).astype(F32)

    def step(k, carry):
        rows = work[k]
        shift = lax.rem(width - k * size, width)
        diagonal = pltpu.roll(rows[:, :width], shift, 1)[:, :size]
        small = small_inverse_factor(diagonal)
        upper = jnp.dot(small, rows, precision=lax.Precision.HIGHEST, preferred_element_type=F32)
        out[k] = upper[:, width:]
        left = jnp.where(lane >= (k + 1) * size, upper[:, :width], 0.0)
        update = lax.dot_general(
            left, upper, (((0,), (0,)), ((), ())),
            precision=lax.Precision.HIGHEST, preferred_element_type=F32,
        )
        for i in range(blocks):
            work[i] -= update[i * size : (i + 1) * size]
        return carry

    lax.fori_loop(0, blocks, step, 0)


def gram_kernel(
    n_obs, n_par, center, lower, upper, full, inverse,
    sample, from_low, from_high, gram, work, hs, hr, rs, rr, send1, got1, send2, got2, *sems,
):
    o, p = lax.axis_index("obs"), lax.axis_index("par")
    devices = groups(n_obs, n_par, o, p)
    count = n_obs * n_par
    order = p * n_obs + o
    rows = center.shape[0]
    before = lax.rem(order + count - 1, count)
    after = lax.rem(order + 1, count)
    below = (lax.rem(before, n_obs), before // n_obs)
    above = (lax.rem(after, n_obs), after // n_obs)
    greet(devices[0] + devices[1] + [below, above])
    down = remote(lower, from_high, hs.at[0], hr.at[0], below)
    up = remote(upper, from_low, hs.at[1], hr.at[1], above)

    @pl.when(order > 0)
    def _():
        down.start()

    @pl.when(order < count - 1)
    def _():
        up.start()

    sample[...] = center[...]

    @pl.when(order > 0)
    def _():
        down.wait_send()
        up.wait_recv()
        sample[pl.ds(0, HALO), :] += from_low[...].astype(F32)

    @pl.when(order < count - 1)
    def _():
        up.wait_send()
        down.wait_recv()
        sample[pl.ds(rows - HALO, HALO), :] += from_high[...].astype(F32)

    full[o] = sample[...].astype(BF16)
    value = lax.dot_general(
        sample[...], sample[...], (((0,), (0,)), ((), ())),
        precision=lax.Precision.HIGHEST, preferred_element_type=F32,
    ) / (rows * count)
    sum_everywhere(o, p, devices, value, send1, got1, send2, got2, gram, sems)
    spread = spread_out(full.at[o], devices[0], rs, rr)
    matrix = jnp.concatenate(
        [gram[i, q] for i in range(n_obs) for q in range(n_par)], axis=0
    )
    inverse_factor(matrix, work, inverse, inverse.shape[1])
    for copy in spread:
        copy.wait()


def second_kernel(
    n_obs, n_par, offs, basis, coeffs, jac, image, ritz,
    low, high, values, held, jac_held, ls, part, got, total, hs, hr, ps, pr,
    send1, got1, send2, got2, *sems,
):
    o, p = lax.axis_index("obs"), lax.axis_index("par")
    loads = fetch(basis, coeffs, jac, values, held, jac_held, low, high, ls)
    devices = groups(n_obs, n_par, o, p)
    greet(devices[0] + devices[1])
    mine = image_and_parts(
        n_par, o, p, offs, basis, loads, values, held, jac_held, image, low, high,
        part, got, hs, hr, ps, pr,
    )
    value = lax.dot_general(
        mine, mine, (((0,), (0,)), ((), ())),
        precision=lax.Precision.HIGHEST, preferred_element_type=F32,
    ) / (jac_held.shape[0] * n_obs)
    sum_everywhere(o, p, devices, value, send1, got1, send2, got2, total, sems)
    piece = total.shape[2]
    for i in range(n_obs):
        for q in range(n_par):
            start = (i * n_par + q) * piece
            ritz[start : start + piece, :] = total[i, q].astype(F32)


def dma(count):
    return pltpu.SemaphoreType.DMA((count,))


def params(collective):
    return pltpu.CompilerParams(
        collective_id=collective, has_side_effects=True, vmem_limit_bytes=LIMIT
    )


def body(n_obs, n_par, jacobian, probes, coeffs, offsets):
    obs, rows = jacobian.shape
    width = probes.shape[1]
    own = rows // n_obs
    count = n_obs * n_par
    halos = [pltpu.VMEM((3 * REACH, BLK, width), BF16)] * 2 + [
        pltpu.VMEM((rows // BLK, BLK, width), BF16),
        pltpu.VMEM(coeffs.shape, BF16),
        pltpu.VMEM((obs, rows), BF16),
        dma(5),
    ]
    anywhere = pl.BlockSpec(memory_space=pl.ANY)
    parts = [pltpu.VMEM((n_par, obs // n_par, width), BF16)] * 2
    adjoint = pl.pallas_call(
        functools.partial(first_kernel, n_obs, n_par),
        out_shape=jax.ShapeDtypeStruct((own, width), BF16),
        in_specs=[SMEM, anywhere, anywhere, anywhere],
        out_specs=VMEM,
        scratch_shapes=halos
        + [pltpu.VMEM((rows, width), BF16)]
        + parts
        + [pltpu.VMEM((n_par, obs // n_par, width), BF16)]
        + [pltpu.VMEM((n_obs, own, width), BF16)] * 2
        + [dma(2)] * 2
        + [dma(n_par)] * 4
        + [dma(n_obs)] * 2,
        compiler_params=params(0),
        name="first_pass",
    )(offsets, probes.reshape(-1, BLK, width), coeffs, jacobian)
    center, lower, upper = pl.pallas_call(
        adjoint_kernel,
        out_shape=[
            jax.ShapeDtypeStruct((own, width), F32),
            jax.ShapeDtypeStruct((HALO, width), BF16),
            jax.ShapeDtypeStruct((HALO, width), BF16),
        ],
        in_specs=[SMEM, VMEM, pl.BlockSpec(memory_space=pl.ANY)],
        out_specs=[VMEM] * 3,
        scratch_shapes=[
            pltpu.VMEM((own + 2 * HALO, width), F32),
            pltpu.VMEM((own // BLK,) + coeffs.shape[1:], BF16),
            dma(1),
        ],
        compiler_params=pltpu.CompilerParams(vmem_limit_bytes=LIMIT),
        name="adjoint_prior",
    )(offsets, adjoint, coeffs)
    block = 64
    full, inverse = pl.pallas_call(
        functools.partial(gram_kernel, n_obs, n_par),
        out_shape=[
            jax.ShapeDtypeStruct((n_obs, own, width), BF16),
            jax.ShapeDtypeStruct((width // block, block, width), F32),
        ],
        in_specs=[VMEM] * 3,
        out_specs=[VMEM] * 2,
        scratch_shapes=[pltpu.VMEM((own, width), F32)]
        + [pltpu.VMEM((HALO, width), BF16)] * 2
        + [pltpu.VMEM((n_obs, n_par, width // count, width), F32)]
        + [pltpu.VMEM((width // block, block, 2 * width), F32)]
        + [dma(2)] * 2
        + [dma(n_obs)] * 2
        + sum_scratch(n_obs, n_par, width, F32),
        compiler_params=params(1),
        name="gram",
    )(center, lower, upper)
    inverse = inverse.reshape(width, width)
    high_part = inverse.astype(BF16)
    low_part = (inverse - high_part.astype(F32)).astype(BF16)
    sample = full.reshape(rows, width)
    last = (((1,), (1,)), ((), ()))
    basis = (
        lax.dot_general(sample, high_part, last, preferred_element_type=F32)
        + lax.dot_general(sample, low_part, last, preferred_element_type=F32)
    ).astype(BF16)
    image, ritz = pl.pallas_call(
        functools.partial(second_kernel, n_obs, n_par),
        out_shape=[
            jax.ShapeDtypeStruct((rows, width), BF16),
            jax.ShapeDtypeStruct((width, width), F32),
        ],
        in_specs=[SMEM, anywhere, anywhere, anywhere],
        out_specs=[VMEM] * 2,
        scratch_shapes=halos
        + parts
        + [pltpu.VMEM((n_obs, n_par, width // count, width), BF16)]
        + [dma(2)] * 2
        + [dma(n_par)] * 2
        + sum_scratch(n_obs, n_par, width, BF16),
        compiler_params=params(2),
        name="second_pass",
    )(offsets, basis.reshape(-1, BLK, width), coeffs, jacobian)
    return basis, image, ritz


def solution(mesh):
    return jax.shard_map(
        functools.partial(body, mesh.shape["obs"], mesh.shape["par"]),
        mesh=mesh,
        in_specs=(P("obs", "par"), P("par", None), P("par", None, None, None), P("par", None)),
        out_specs=(P("par", None), P("par", None), P()),
        check_vma=False,
    )
```

```python
import functools

import jax
import jax.numpy as jnp
from jax import lax
from jax.experimental import pallas as pl
from jax.experimental.pallas import tpu as pltpu
from jax.sharding import PartitionSpec as P

BLK = 128
REACH = 4
HALO = REACH * BLK
MESH = pl.DeviceIdType.MESH
F32 = jnp.float32
BF16 = jnp.bfloat16
VMEM = pl.BlockSpec(memory_space=pltpu.VMEM)
SMEM = pl.BlockSpec(memory_space=pltpu.SMEM)
LIMIT = 60 * 1024 * 1024


def greet(devices):
    barrier = pltpu.get_barrier_semaphore()
    for device in devices:
        pl.semaphore_signal(barrier, inc=1, device_id=device, device_id_type=MESH)
    pl.semaphore_wait(barrier, len(devices))


def remote(src, dst, send, recv, device):
    return pltpu.make_async_remote_copy(
        src_ref=src, dst_ref=dst, send_sem=send, recv_sem=recv, device_id=device, device_id_type=MESH
    )


def prior_block(b, base, source, coeffs, offs):
    def pick(offset):
        return source[b - base + offset]

    left = jnp.concatenate([coeffs[b, 0], coeffs[b, 1], coeffs[b, 2]], axis=1)
    right = jnp.concatenate([pick(0), pick(offs[b, 0]), pick(offs[b, 1])], axis=0)
    return jnp.dot(left, right, preferred_element_type=F32).astype(BF16)


def fetch(source, coeffs, jac, values, held, jac_held, low, high, sem):
    blocks = source.shape[0]
    side = 2 * REACH
    loads = [
        pltpu.make_async_copy(source, values, sem.at[0]),
        pltpu.make_async_copy(coeffs, held, sem.at[1]),
        pltpu.make_async_copy(source.at[pl.ds(0, side)], low.at[pl.ds(REACH, side)], sem.at[2]),
        pltpu.make_async_copy(source.at[pl.ds(blocks - side, side)], high.at[pl.ds(0, side)], sem.at[3]),
        pltpu.make_async_copy(jac, jac_held, sem.at[4]),
    ]
    for load in loads:
        load.start()
    return loads


def image_and_parts(
    n_par, o, p, offs, source, loads, values, coeffs, jac, image, low, high, part, got, hs, hr, ps, pr
):
    blocks = values.shape[0]
    side = 2 * REACH
    below = lax.rem(p + n_par - 1, n_par)
    above = lax.rem(p + 1, n_par)
    down = remote(source.at[pl.ds(0, REACH)], high.at[pl.ds(side, REACH)], hs.at[0], hr.at[0], (o, below))
    up = remote(source.at[pl.ds(blocks - REACH, REACH)], low.at[pl.ds(0, REACH)], hs.at[1], hr.at[1], (o, above))

    @pl.when(p > 0)
    def _():
        down.start()

    @pl.when(p < n_par - 1)
    def _():
        up.start()

    @pl.when(p == 0)
    def _():
        low[pl.ds(0, REACH)] = jnp.zeros((REACH,) + low.shape[1:], BF16)

    @pl.when(p == n_par - 1)
    def _():
        high[pl.ds(side, REACH)] = jnp.zeros((REACH,) + high.shape[1:], BF16)

    loads[0].wait()
    loads[1].wait()

    def inner(b, carry):
        image[pl.ds(pl.multiple_of(b * BLK, BLK), BLK), :] = prior_block(b, 0, values, coeffs, offs)
        return carry

    lax.fori_loop(REACH, blocks - REACH, inner, 0, unroll=4)

    @pl.when(p > 0)
    def _():
        down.wait_send()
        up.wait_recv()

    @pl.when(p < n_par - 1)
    def _():
        up.wait_send()
        down.wait_recv()

    loads[2].wait()
    loads[3].wait()
    for b in range(REACH):
        image[pl.ds(b * BLK, BLK), :] = prior_block(b, -REACH, low, coeffs, offs)
    for b in range(blocks - REACH, blocks):
        image[pl.ds(b * BLK, BLK), :] = prior_block(b, blocks - 2 * REACH, high, coeffs, offs)

    loads[4].wait()
    total = jnp.dot(jac[...], image[...], preferred_element_type=F32)
    piece = part.shape[1]
    for q in range(n_par):
        part[q] = total[q * piece : (q + 1) * piece].astype(BF16)
    copies = []
    for d in range(1, n_par):
        q = lax.rem(p + d, n_par)
        copy = remote(part.at[q], got.at[d], ps.at[d], pr.at[d], (o, q))
        copy.start()
        copies.append(copy)
    mine = part[p].astype(F32)
    for d in range(1, n_par):
        copies[d - 1].wait()
        mine = mine + got[d].astype(F32)
    return mine


def first_kernel(
    n_obs, n_par, offs, probes, coeffs, jac_ref, out,
    low, high, values, held, jac, ls, image, part, got, fwd, adj, adj_got, hs, hr, ps, pr, gs, gr, os, orr,
):
    o, p = lax.axis_index("obs"), lax.axis_index("par")
    loads = fetch(probes, coeffs, jac_ref, values, held, jac, low, high, ls)
    greet(
        [(o, lax.rem(p + d, n_par)) for d in range(1, n_par)]
        + [(lax.rem(o + d, n_obs), p) for d in range(1, n_obs)]
    )
    mine = image_and_parts(
        n_par, o, p, offs, probes, loads, values, held, jac, image, low, high,
        part, got, hs, hr, ps, pr,
    )
    fwd[p] = mine.astype(BF16)
    copies = []
    for d in range(1, n_par):
        copy = remote(fwd.at[p], fwd.at[p], gs.at[d], gr.at[d], (o, lax.rem(p + d, n_par)))
        copy.start()
        copies.append(copy)
    for copy in copies:
        copy.wait()
    forward = fwd[...].reshape(jac.shape[0], fwd.shape[2])
    rows = adj.shape[1]
    tile = 256
    copies = []
    for d in list(range(1, n_obs)) + [0]:
        q = lax.rem(o + d, n_obs)

        def step(t, carry):
            start = pl.multiple_of(q * rows + t * tile, tile)
            value = lax.dot_general(
                jac[:, pl.ds(start, tile)], forward, (((0,), (0,)), ((), ())), preferred_element_type=F32
            )
            adj[d, pl.ds(pl.multiple_of(t * tile, tile), tile), :] = value.astype(BF16)
            return carry

        lax.fori_loop(0, rows // tile, step, 0)
        if d:
            copy = remote(adj.at[d], adj_got.at[d], os.at[d], orr.at[d], (q, p))
            copy.start()
            copies.append(copy)
    total = adj[0].astype(F32)
    for d in range(1, n_obs):
        copies[d - 1].wait()
        total = total + adj_got[d].astype(F32)
    out[...] = total.astype(BF16)


def adjoint_kernel(offs, values, coeffs, center, lower, upper, acc, held, sem):
    o = lax.axis_index("obs")
    blocks = values.shape[0] // BLK
    width = values.shape[1]
    load = pltpu.make_async_copy(coeffs.at[pl.ds(o * blocks, blocks)], held, sem.at[0])
    load.start()
    acc[...] = jnp.zeros_like(acc)
    load.wait()
    for b in range(blocks):
        v = values[pl.ds(b * BLK, BLK), :]
        for j in range(3):
            offset = 0 if j == 0 else offs[o * blocks + b, j - 1]
            where = pl.ds(pl.multiple_of((b + REACH + offset) * BLK, BLK), BLK)
            acc[where, :] += lax.dot_general(
                held[b, j], v, (((0,), (0,)), ((), ())), preferred_element_type=F32
            )
    lower[...] = acc[pl.ds(0, HALO), :].astype(BF16)
    center[...] = acc[pl.ds(HALO, blocks * BLK), :]
    upper[...] = acc[pl.ds(HALO + blocks * BLK, HALO), :].astype(BF16)


def groups(n_obs, n_par, o, p):
    along_obs = [(lax.rem(o + d, n_obs), p) for d in range(1, n_obs)]
    along_par = [(o, lax.rem(p + d, n_par)) for d in range(1, n_par)]
    return along_obs, along_par


def swap(send, got, index, devices, send_sem, recv_sem):
    copies = []
    for d, device in enumerate(devices, 1):
        copy = remote(send.at[device[index]], got.at[d], send_sem.at[d], recv_sem.at[d], device)
        copy.start()
        copies.append(copy)
    return copies


def spread_out(ref, devices, send_sem, recv_sem):
    copies = []
    for d, device in enumerate(devices, 1):
        copy = remote(ref, ref, send_sem.at[d], recv_sem.at[d], device)
        copy.start()
        copies.append(copy)
    return copies


def sum_everywhere(o, p, devices, value, send1, got1, send2, got2, out, sems, beside=None):
    along_obs, along_par = devices
    n_obs, n_par, piece, _ = out.shape
    kind = out.dtype
    tall = n_par * piece
    for q in range(n_obs):
        send1[q] = value[q * tall : (q + 1) * tall].astype(kind)
    copies = swap(send1, got1, 0, along_obs, sems[0], sems[1])
    mine = send1[o].astype(F32)
    for d, copy in enumerate(copies, 1):
        copy.wait()
        mine = mine + got1[d].astype(F32)
    if beside is not None:
        beside()
    for q in range(n_par):
        send2[q] = mine[q * piece : (q + 1) * piece].astype(kind)
    copies = swap(send2, got2, 1, along_par, sems[2], sems[3])
    mine = send2[p].astype(F32)
    for d, copy in enumerate(copies, 1):
        copy.wait()
        mine = mine + got2[d].astype(F32)
    out[o, p] = mine.astype(kind)
    for copy in spread_out(out.at[o, p], along_par, sems[4], sems[5]):
        copy.wait()
    for copy in spread_out(out.at[o], along_obs, sems[6], sems[7]):
        copy.wait()


def sum_scratch(n_obs, n_par, width, kind):
    tall = width // n_obs
    return (
        [pltpu.VMEM((n_obs, tall, width), kind)] * 2
        + [pltpu.VMEM((n_par, tall // n_par, width), kind)] * 2
        + [dma(n_obs)] * 2
        + [dma(n_par)] * 4
        + [dma(n_obs)] * 2
    )


def small_inverse_factor(matrix):
    size = matrix.shape[0]
    row = lax.broadcasted_iota(jnp.int32, (size, size), 0)
    lane = lax.broadcasted_iota(jnp.int32, (size, size), 1)
    work = jnp.concatenate([matrix, (row == lane).astype(F32)], axis=1)
    group = 8
    parts = [work[g : g + group] for g in range(0, size, group)]
    index = lax.broadcasted_iota(jnp.int32, (group, 2 * size), 0)
    scales = []
    for first in range(size // group):
        start = first * group
        columns = [
            [jnp.broadcast_to(part[:, start + t : start + t + 1], part.shape) for part in parts[first:]]
            for t in range(group)
        ]
        for t in range(group):
            pivot = columns[t][0][t : t + 1]
            scales.append(lax.rsqrt(pivot))
            reciprocal = 1.0 / pivot
            scaled = parts[first][t : t + 1] * reciprocal
            columns[t][0] = jnp.where(index > t, columns[t][0], 0.0)
            for u in range(t + 1, group):
                ratio = columns[u][0][t : t + 1] * reciprocal
                columns[u] = [c - e * ratio for c, e in zip(columns[u], columns[t])]
            for g, column in enumerate(columns[t]):
                parts[first + g] = parts[first + g] - column * scaled
    rows = [parts[j // group][j % group : j % group + 1] * scales[j] for j in range(size)]
    return jnp.concatenate(rows, axis=0)[:, size:]


def inverse_factor(gram, work, out, size):
    blocks = work.shape[0]
    width = blocks * size
    row = lax.broadcasted_iota(jnp.int32, (size, width), 0)
    lane = lax.broadcasted_iota(jnp.int32, (size, width), 1)
    for k in range(blocks):
        work[k, :, pl.ds(0, width)] = gram[k * size : (k + 1) * size]
        work[k, :, pl.ds(width, width)] = (lane == row + k * size).astype(F32)

    def step(k, carry):
        rows = work[k]
        shift = lax.rem(width - k * size, width)
        diagonal = pltpu.roll(rows[:, :width], shift, 1)[:, :size]
        small = small_inverse_factor(diagonal)
        upper = jnp.dot(small, rows, precision=lax.Precision.HIGHEST, preferred_element_type=F32)
        out[k] = upper[:, width:]
        left = jnp.where(lane >= (k + 1) * size, upper[:, :width], 0.0)
        update = lax.dot_general(
            left, upper, (((0,), (0,)), ((), ())),
            precision=lax.Precision.HIGHEST, preferred_element_type=F32,
        )
        for i in range(blocks):
            work[i] -= update[i * size : (i + 1) * size]
        return carry

    lax.fori_loop(0, blocks, step, 0)


def gram_kernel(
    n_obs, n_par, center, lower, upper, full, inverse,
    sample, from_low, from_high, gram, work, hs, hr, rs, rr, send1, got1, send2, got2, *sems,
):
    o, p = lax.axis_index("obs"), lax.axis_index("par")
    devices = groups(n_obs, n_par, o, p)
    count = n_obs * n_par
    order = p * n_obs + o
    rows = center.shape[0]
    before = lax.rem(order + count - 1, count)
    after = lax.rem(order + 1, count)
    below = (lax.rem(before, n_obs), before // n_obs)
    above = (lax.rem(after, n_obs), after // n_obs)
    greet(devices[0] + devices[1] + [below, above])
    down = remote(lower, from_high, hs.at[0], hr.at[0], below)
    up = remote(upper, from_low, hs.at[1], hr.at[1], above)

    @pl.when(order > 0)
    def _():
        down.start()

    @pl.when(order < count - 1)
    def _():
        up.start()

    sample[...] = center[...]

    @pl.when(order > 0)
    def _():
        down.wait_send()
        up.wait_recv()
        sample[pl.ds(0, HALO), :] += from_low[...].astype(F32)

    @pl.when(order < count - 1)
    def _():
        up.wait_send()
        down.wait_recv()
        sample[pl.ds(rows - HALO, HALO), :] += from_high[...].astype(F32)

    full[o] = sample[...].astype(BF16)
    value = lax.dot_general(
        sample[...], sample[...], (((0,), (0,)), ((), ())),
        precision=lax.Precision.HIGHEST, preferred_element_type=F32,
    ) / (rows * count)
    spread = []
    half = rows // 2

    def send_half(h):
        spread.extend(
            spread_out(full.at[o, pl.ds(h * half, half)], devices[0], rs.at[h], rr.at[h])
        )

    sum_everywhere(
        o, p, devices, value, send1, got1, send2, got2, gram, sems, lambda: send_half(0)
    )
    send_half(1)
    matrix = jnp.concatenate(
        [gram[i, q] for i in range(n_obs) for q in range(n_par)], axis=0
    )
    inverse_factor(matrix, work, inverse, inverse.shape[1])
    for copy in spread:
        copy.wait()


def second_kernel(
    n_obs, n_par, offs, basis, coeffs, jac, image, ritz,
    low, high, values, held, jac_held, ls, part, got, total, hs, hr, ps, pr,
    send1, got1, send2, got2, *sems,
):
    o, p = lax.axis_index("obs"), lax.axis_index("par")
    loads = fetch(basis, coeffs, jac, values, held, jac_held, low, high, ls)
    devices = groups(n_obs, n_par, o, p)
    greet(devices[0] + devices[1])
    mine = image_and_parts(
        n_par, o, p, offs, basis, loads, values, held, jac_held, image, low, high,
        part, got, hs, hr, ps, pr,
    )
    value = lax.dot_general(
        mine, mine, (((0,), (0,)), ((), ())),
        precision=lax.Precision.HIGHEST, preferred_element_type=F32,
    ) / (jac_held.shape[0] * n_obs)
    sum_everywhere(o, p, devices, value, send1, got1, send2, got2, total, sems)
    piece = total.shape[2]
    for i in range(n_obs):
        for q in range(n_par):
            start = (i * n_par + q) * piece
            ritz[start : start + piece, :] = total[i, q].astype(F32)


def dma(count):
    return pltpu.SemaphoreType.DMA((count,))


def params(collective):
    return pltpu.CompilerParams(
        collective_id=collective, has_side_effects=True, vmem_limit_bytes=LIMIT
    )


def body(n_obs, n_par, jacobian, probes, coeffs, offsets):
    obs, rows = jacobian.shape
    width = probes.shape[1]
    own = rows // n_obs
    count = n_obs * n_par
    halos = [pltpu.VMEM((3 * REACH, BLK, width), BF16)] * 2 + [
        pltpu.VMEM((rows // BLK, BLK, width), BF16),
        pltpu.VMEM(coeffs.shape, BF16),
        pltpu.VMEM((obs, rows), BF16),
        dma(5),
    ]
    anywhere = pl.BlockSpec(memory_space=pl.ANY)
    parts = [pltpu.VMEM((n_par, obs // n_par, width), BF16)] * 2
    adjoint = pl.pallas_call(
        functools.partial(first_kernel, n_obs, n_par),
        out_shape=jax.ShapeDtypeStruct((own, width), BF16),
        in_specs=[SMEM, anywhere, anywhere, anywhere],
        out_specs=VMEM,
        scratch_shapes=halos
        + [pltpu.VMEM((rows, width), BF16)]
        + parts
        + [pltpu.VMEM((n_par, obs // n_par, width), BF16)]
        + [pltpu.VMEM((n_obs, own, width), BF16)] * 2
        + [dma(2)] * 2
        + [dma(n_par)] * 4
        + [dma(n_obs)] * 2,
        compiler_params=params(0),
        name="first_pass",
    )(offsets, probes.reshape(-1, BLK, width), coeffs, jacobian)
    center, lower, upper = pl.pallas_call(
        adjoint_kernel,
        out_shape=[
            jax.ShapeDtypeStruct((own, width), F32),
            jax.ShapeDtypeStruct((HALO, width), BF16),
            jax.ShapeDtypeStruct((HALO, width), BF16),
        ],
        in_specs=[SMEM, VMEM, pl.BlockSpec(memory_space=pl.ANY)],
        out_specs=[VMEM] * 3,
        scratch_shapes=[
            pltpu.VMEM((own + 2 * HALO, width), F32),
            pltpu.VMEM((own // BLK,) + coeffs.shape[1:], BF16),
            dma(1),
        ],
        compiler_params=pltpu.CompilerParams(vmem_limit_bytes=LIMIT),
        name="adjoint_prior",
    )(offsets, adjoint, coeffs)
    block = 64
    full, inverse = pl.pallas_call(
        functools.partial(gram_kernel, n_obs, n_par),
        out_shape=[
            jax.ShapeDtypeStruct((n_obs, own, width), BF16),
            jax.ShapeDtypeStruct((width // block, block, width), F32),
        ],
        in_specs=[VMEM] * 3,
        out_specs=[VMEM] * 2,
        scratch_shapes=[pltpu.VMEM((own, width), F32)]
        + [pltpu.VMEM((HALO, width), BF16)] * 2
        + [pltpu.VMEM((n_obs, n_par, width // count, width), F32)]
        + [pltpu.VMEM((width // block, block, 2 * width), F32)]
        + [dma(2)] * 2
        + [pltpu.SemaphoreType.DMA((2, n_obs))] * 2
        + sum_scratch(n_obs, n_par, width, F32),
        compiler_params=params(1),
        name="gram",
    )(center, lower, upper)
    inverse = inverse.reshape(width, width)
    high_part = inverse.astype(BF16)
    low_part = (inverse - high_part.astype(F32)).astype(BF16)
    sample = full.reshape(rows, width)
    last = (((1,), (1,)), ((), ()))
    basis = (
        lax.dot_general(sample, high_part, last, preferred_element_type=F32)
        + lax.dot_general(sample, low_part, last, preferred_element_type=F32)
    ).astype(BF16)
    image, ritz = pl.pallas_call(
        functools.partial(second_kernel, n_obs, n_par),
        out_shape=[
            jax.ShapeDtypeStruct((rows, width), BF16),
            jax.ShapeDtypeStruct((width, width), F32),
        ],
        in_specs=[SMEM, anywhere, anywhere, anywhere],
        out_specs=[VMEM] * 2,
        scratch_shapes=halos
        + parts
        + [pltpu.VMEM((n_obs, n_par, width // count, width), BF16)]
        + [dma(2)] * 2
        + [dma(n_par)] * 2
        + sum_scratch(n_obs, n_par, width, BF16),
        compiler_params=params(2),
        name="second_pass",
    )(offsets, basis.reshape(-1, BLK, width), coeffs, jacobian)
    return basis, image, ritz


def solution(mesh):
    return jax.shard_map(
        functools.partial(body, mesh.shape["obs"], mesh.shape["par"]),
        mesh=mesh,
        in_specs=(P("obs", "par"), P("par", None), P("par", None, None, None), P("par", None)),
        out_specs=(P("par", None), P("par", None), P()),
        check_vma=False,
    )
```

```python
import functools

import jax
import jax.numpy as jnp
from jax import lax
from jax.experimental import pallas as pl
from jax.experimental.pallas import tpu as pltpu
from jax.sharding import PartitionSpec as P

BLK = 128
REACH = 4
HALO = REACH * BLK
MESH = pl.DeviceIdType.MESH
F32 = jnp.float32
BF16 = jnp.bfloat16
VMEM = pl.BlockSpec(memory_space=pltpu.VMEM)
SMEM = pl.BlockSpec(memory_space=pltpu.SMEM)
LIMIT = 60 * 1024 * 1024


def greet(devices):
    barrier = pltpu.get_barrier_semaphore()
    for device in devices:
        pl.semaphore_signal(barrier, inc=1, device_id=device, device_id_type=MESH)
    pl.semaphore_wait(barrier, len(devices))


def remote(src, dst, send, recv, device):
    return pltpu.make_async_remote_copy(
        src_ref=src, dst_ref=dst, send_sem=send, recv_sem=recv, device_id=device, device_id_type=MESH
    )


def prior_block(b, base, source, coeffs, offs):
    def pick(offset):
        return source[b - base + offset]

    left = jnp.concatenate([coeffs[b, 0], coeffs[b, 1], coeffs[b, 2]], axis=1)
    right = jnp.concatenate([pick(0), pick(offs[b, 0]), pick(offs[b, 1])], axis=0)
    return jnp.dot(left, right, preferred_element_type=F32).astype(BF16)


def fetch(source, coeffs, jac, values, held, jac_held, low, high, sem):
    blocks = source.shape[0]
    side = 2 * REACH
    loads = [
        pltpu.make_async_copy(source, values, sem.at[0]),
        pltpu.make_async_copy(coeffs, held, sem.at[1]),
        pltpu.make_async_copy(source.at[pl.ds(0, side)], low.at[pl.ds(REACH, side)], sem.at[2]),
        pltpu.make_async_copy(source.at[pl.ds(blocks - side, side)], high.at[pl.ds(0, side)], sem.at[3]),
        pltpu.make_async_copy(jac, jac_held, sem.at[4]),
    ]
    for load in loads:
        load.start()
    return loads


def image_and_parts(
    n_par, o, p, offs, source, loads, values, coeffs, jac, image, low, high, part, got, hs, hr, ps, pr
):
    blocks = values.shape[0]
    side = 2 * REACH
    below = lax.rem(p + n_par - 1, n_par)
    above = lax.rem(p + 1, n_par)
    down = remote(source.at[pl.ds(0, REACH)], high.at[pl.ds(side, REACH)], hs.at[0], hr.at[0], (o, below))
    up = remote(source.at[pl.ds(blocks - REACH, REACH)], low.at[pl.ds(0, REACH)], hs.at[1], hr.at[1], (o, above))

    @pl.when(p > 0)
    def _():
        down.start()

    @pl.when(p < n_par - 1)
    def _():
        up.start()

    @pl.when(p == 0)
    def _():
        low[pl.ds(0, REACH)] = jnp.zeros((REACH,) + low.shape[1:], BF16)

    @pl.when(p == n_par - 1)
    def _():
        high[pl.ds(side, REACH)] = jnp.zeros((REACH,) + high.shape[1:], BF16)

    loads[0].wait()
    loads[1].wait()

    def inner(b, carry):
        image[pl.ds(pl.multiple_of(b * BLK, BLK), BLK), :] = prior_block(b, 0, values, coeffs, offs)
        return carry

    lax.fori_loop(REACH, blocks - REACH, inner, 0, unroll=4)

    @pl.when(p > 0)
    def _():
        down.wait_send()
        up.wait_recv()

    @pl.when(p < n_par - 1)
    def _():
        up.wait_send()
        down.wait_recv()

    loads[2].wait()
    loads[3].wait()
    for b in range(REACH):
        image[pl.ds(b * BLK, BLK), :] = prior_block(b, -REACH, low, coeffs, offs)
    for b in range(blocks - REACH, blocks):
        image[pl.ds(b * BLK, BLK), :] = prior_block(b, blocks - 2 * REACH, high, coeffs, offs)

    loads[4].wait()
    piece = part.shape[1]
    half = n_par // 2

    def to(q, d):
        return remote(part.at[q], got.at[d], ps.at[d], pr.at[d], (o, q))

    for first in (0, half):
        total = jnp.dot(
            jac[first * piece : (first + half) * piece, :], image[...], preferred_element_type=F32
        )
        for q in range(half):
            part[first + q] = total[q * piece : (q + 1) * piece].astype(BF16)
        for q in range(first, first + half):

            @pl.when(p != q)
            def _():
                to(q, lax.rem(q - p + n_par, n_par)).start()

    copies = [to(lax.rem(p + d, n_par), d) for d in range(1, n_par)]
    mine = part[p].astype(F32)
    for d in range(1, n_par):
        copies[d - 1].wait()
        mine = mine + got[d].astype(F32)
    return mine


def first_kernel(
    n_obs, n_par, offs, probes, coeffs, jac_ref, out,
    low, high, values, held, jac, ls, image, part, got, fwd, adj, adj_got, hs, hr, ps, pr, gs, gr, os, orr,
):
    o, p = lax.axis_index("obs"), lax.axis_index("par")
    loads = fetch(probes, coeffs, jac_ref, values, held, jac, low, high, ls)
    greet(
        [(o, lax.rem(p + d, n_par)) for d in range(1, n_par)]
        + [(lax.rem(o + d, n_obs), p) for d in range(1, n_obs)]
    )
    mine = image_and_parts(
        n_par, o, p, offs, probes, loads, values, held, jac, image, low, high,
        part, got, hs, hr, ps, pr,
    )
    fwd[p] = mine.astype(BF16)
    copies = []
    for d in range(1, n_par):
        copy = remote(fwd.at[p], fwd.at[p], gs.at[d], gr.at[d], (o, lax.rem(p + d, n_par)))
        copy.start()
        copies.append(copy)
    for copy in copies:
        copy.wait()
    forward = fwd[...].reshape(jac.shape[0], fwd.shape[2])
    rows = adj.shape[1]
    tile = 256
    copies = []
    for d in list(range(1, n_obs)) + [0]:
        q = lax.rem(o + d, n_obs)

        def step(t, carry):
            start = pl.multiple_of(q * rows + t * tile, tile)
            value = lax.dot_general(
                jac[:, pl.ds(start, tile)], forward, (((0,), (0,)), ((), ())), preferred_element_type=F32
            )
            adj[d, pl.ds(pl.multiple_of(t * tile, tile), tile), :] = value.astype(BF16)
            return carry

        lax.fori_loop(0, rows // tile, step, 0)
        if d:
            copy = remote(adj.at[d], adj_got.at[d], os.at[d], orr.at[d], (q, p))
            copy.start()
            copies.append(copy)
    total = adj[0].astype(F32)
    for d in range(1, n_obs):
        copies[d - 1].wait()
        total = total + adj_got[d].astype(F32)
    out[...] = total.astype(BF16)


def adjoint_kernel(offs, values, coeffs, center, lower, upper, acc, held, sem):
    o = lax.axis_index("obs")
    blocks = values.shape[0] // BLK
    width = values.shape[1]
    load = pltpu.make_async_copy(coeffs.at[pl.ds(o * blocks, blocks)], held, sem.at[0])
    load.start()
    acc[...] = jnp.zeros_like(acc)
    load.wait()
    for b in range(blocks):
        v = values[pl.ds(b * BLK, BLK), :]
        for j in range(3):
            offset = 0 if j == 0 else offs[o * blocks + b, j - 1]
            where = pl.ds(pl.multiple_of((b + REACH + offset) * BLK, BLK), BLK)
            acc[where, :] += lax.dot_general(
                held[b, j], v, (((0,), (0,)), ((), ())), preferred_element_type=F32
            )
    lower[...] = acc[pl.ds(0, HALO), :].astype(BF16)
    center[...] = acc[pl.ds(HALO, blocks * BLK), :]
    upper[...] = acc[pl.ds(HALO + blocks * BLK, HALO), :].astype(BF16)


def groups(n_obs, n_par, o, p):
    along_obs = [(lax.rem(o + d, n_obs), p) for d in range(1, n_obs)]
    along_par = [(o, lax.rem(p + d, n_par)) for d in range(1, n_par)]
    return along_obs, along_par


def swap(send, got, index, devices, send_sem, recv_sem):
    copies = []
    for d, device in enumerate(devices, 1):
        copy = remote(send.at[device[index]], got.at[d], send_sem.at[d], recv_sem.at[d], device)
        copy.start()
        copies.append(copy)
    return copies


def spread_out(ref, devices, send_sem, recv_sem):
    copies = []
    for d, device in enumerate(devices, 1):
        copy = remote(ref, ref, send_sem.at[d], recv_sem.at[d], device)
        copy.start()
        copies.append(copy)
    return copies


def sum_everywhere(o, p, devices, value, send1, got1, send2, got2, out, sems, beside=None):
    along_obs, along_par = devices
    n_obs, n_par, piece, _ = out.shape
    kind = out.dtype
    tall = n_par * piece
    for q in range(n_obs):
        send1[q] = value[q * tall : (q + 1) * tall].astype(kind)
    copies = swap(send1, got1, 0, along_obs, sems[0], sems[1])
    mine = send1[o].astype(F32)
    for d, copy in enumerate(copies, 1):
        copy.wait()
        mine = mine + got1[d].astype(F32)
    if beside is not None:
        beside()
    for q in range(n_par):
        send2[q] = mine[q * piece : (q + 1) * piece].astype(kind)
    copies = swap(send2, got2, 1, along_par, sems[2], sems[3])
    mine = send2[p].astype(F32)
    for d, copy in enumerate(copies, 1):
        copy.wait()
        mine = mine + got2[d].astype(F32)
    out[o, p] = mine.astype(kind)
    for copy in spread_out(out.at[o, p], along_par, sems[4], sems[5]):
        copy.wait()
    for copy in spread_out(out.at[o], along_obs, sems[6], sems[7]):
        copy.wait()


def sum_scratch(n_obs, n_par, width, kind):
    tall = width // n_obs
    return (
        [pltpu.VMEM((n_obs, tall, width), kind)] * 2
        + [pltpu.VMEM((n_par, tall // n_par, width), kind)] * 2
        + [dma(n_obs)] * 2
        + [dma(n_par)] * 4
        + [dma(n_obs)] * 2
    )


def small_inverse_factor(matrix):
    size = matrix.shape[0]
    row = lax.broadcasted_iota(jnp.int32, (size, size), 0)
    lane = lax.broadcasted_iota(jnp.int32, (size, size), 1)
    work = jnp.concatenate([matrix, (row == lane).astype(F32)], axis=1)
    group = 8
    parts = [work[g : g + group] for g in range(0, size, group)]
    index = lax.broadcasted_iota(jnp.int32, (group, 2 * size), 0)
    scales = []
    for first in range(size // group):
        start = first * group
        columns = [
            [jnp.broadcast_to(part[:, start + t : start + t + 1], part.shape) for part in parts[first:]]
            for t in range(group)
        ]
        for t in range(group):
            pivot = columns[t][0][t : t + 1]
            scales.append(lax.rsqrt(pivot))
            reciprocal = 1.0 / pivot
            scaled = parts[first][t : t + 1] * reciprocal
            columns[t][0] = jnp.where(index > t, columns[t][0], 0.0)
            for u in range(t + 1, group):
                ratio = columns[u][0][t : t + 1] * reciprocal
                columns[u] = [c - e * ratio for c, e in zip(columns[u], columns[t])]
            for g, column in enumerate(columns[t]):
                parts[first + g] = parts[first + g] - column * scaled
    rows = [parts[j // group][j % group : j % group + 1] * scales[j] for j in range(size)]
    return jnp.concatenate(rows, axis=0)[:, size:]


def inverse_factor(gram, work, out, size):
    blocks = work.shape[0]
    width = blocks * size
    row = lax.broadcasted_iota(jnp.int32, (size, width), 0)
    lane = lax.broadcasted_iota(jnp.int32, (size, width), 1)
    for k in range(blocks):
        work[k, :, pl.ds(0, width)] = gram[k * size : (k + 1) * size]
        work[k, :, pl.ds(width, width)] = (lane == row + k * size).astype(F32)

    def step(k, carry):
        rows = work[k]
        shift = lax.rem(width - k * size, width)
        diagonal = pltpu.roll(rows[:, :width], shift, 1)[:, :size]
        small = small_inverse_factor(diagonal)
        upper = jnp.dot(small, rows, precision=lax.Precision.HIGHEST, preferred_element_type=F32)
        out[k] = upper[:, width:]
        left = jnp.where(lane >= (k + 1) * size, upper[:, :width], 0.0)
        update = lax.dot_general(
            left, upper, (((0,), (0,)), ((), ())),
            precision=lax.Precision.HIGHEST, preferred_element_type=F32,
        )
        for i in range(blocks):
            work[i] -= update[i * size : (i + 1) * size]
        return carry

    lax.fori_loop(0, blocks, step, 0)


def gram_kernel(
    n_obs, n_par, center, lower, upper, full, inverse,
    sample, from_low, from_high, gram, work, hs, hr, rs, rr, send1, got1, send2, got2, *sems,
):
    o, p = lax.axis_index("obs"), lax.axis_index("par")
    devices = groups(n_obs, n_par, o, p)
    count = n_obs * n_par
    order = p * n_obs + o
    rows = center.shape[0]
    before = lax.rem(order + count - 1, count)
    after = lax.rem(order + 1, count)
    below = (lax.rem(before, n_obs), before // n_obs)
    above = (lax.rem(after, n_obs), after // n_obs)
    greet(devices[0] + devices[1] + [below, above])
    down = remote(lower, from_high, hs.at[0], hr.at[0], below)
    up = remote(upper, from_low, hs.at[1], hr.at[1], above)

    @pl.when(order > 0)
    def _():
        down.start()

    @pl.when(order < count - 1)
    def _():
        up.start()

    sample[...] = center[...]

    @pl.when(order > 0)
    def _():
        down.wait_send()
        up.wait_recv()
        sample[pl.ds(0, HALO), :] += from_low[...].astype(F32)

    @pl.when(order < count - 1)
    def _():
        up.wait_send()
        down.wait_recv()
        sample[pl.ds(rows - HALO, HALO), :] += from_high[...].astype(F32)

    full[o] = sample[...].astype(BF16)
    value = lax.dot_general(
        sample[...], sample[...], (((0,), (0,)), ((), ())),
        precision=lax.Precision.HIGHEST, preferred_element_type=F32,
    ) / (rows * count)
    spread = []
    half = rows // 2

    def send_half(h):
        spread.extend(
            spread_out(full.at[o, pl.ds(h * half, half)], devices[0], rs.at[h], rr.at[h])
        )

    sum_everywhere(
        o, p, devices, value, send1, got1, send2, got2, gram, sems, lambda: send_half(0)
    )
    send_half(1)
    matrix = jnp.concatenate(
        [gram[i, q] for i in range(n_obs) for q in range(n_par)], axis=0
    )
    inverse_factor(matrix, work, inverse, inverse.shape[1])
    for copy in spread:
        copy.wait()


def second_kernel(
    n_obs, n_par, offs, basis, coeffs, jac, image, ritz,
    low, high, values, held, jac_held, ls, part, got, total, hs, hr, ps, pr,
    send1, got1, send2, got2, *sems,
):
    o, p = lax.axis_index("obs"), lax.axis_index("par")
    loads = fetch(basis, coeffs, jac, values, held, jac_held, low, high, ls)
    devices = groups(n_obs, n_par, o, p)
    greet(devices[0] + devices[1])
    mine = image_and_parts(
        n_par, o, p, offs, basis, loads, values, held, jac_held, image, low, high,
        part, got, hs, hr, ps, pr,
    )
    value = lax.dot_general(
        mine, mine, (((0,), (0,)), ((), ())),
        precision=lax.Precision.HIGHEST, preferred_element_type=F32,
    ) / (jac_held.shape[0] * n_obs)
    sum_everywhere(o, p, devices, value, send1, got1, send2, got2, total, sems)
    piece = total.shape[2]
    for i in range(n_obs):
        for q in range(n_par):
            start = (i * n_par + q) * piece
            ritz[start : start + piece, :] = total[i, q].astype(F32)


def dma(count):
    return pltpu.SemaphoreType.DMA((count,))


def params(collective):
    return pltpu.CompilerParams(
        collective_id=collective, has_side_effects=True, vmem_limit_bytes=LIMIT
    )


def body(n_obs, n_par, jacobian, probes, coeffs, offsets):
    obs, rows = jacobian.shape
    width = probes.shape[1]
    own = rows // n_obs
    count = n_obs * n_par
    halos = [pltpu.VMEM((3 * REACH, BLK, width), BF16)] * 2 + [
        pltpu.VMEM((rows // BLK, BLK, width), BF16),
        pltpu.VMEM(coeffs.shape, BF16),
        pltpu.VMEM((obs, rows), BF16),
        dma(5),
    ]
    anywhere = pl.BlockSpec(memory_space=pl.ANY)
    parts = [pltpu.VMEM((n_par, obs // n_par, width), BF16)] * 2
    adjoint = pl.pallas_call(
        functools.partial(first_kernel, n_obs, n_par),
        out_shape=jax.ShapeDtypeStruct((own, width), BF16),
        in_specs=[SMEM, anywhere, anywhere, anywhere],
        out_specs=VMEM,
        scratch_shapes=halos
        + [pltpu.VMEM((rows, width), BF16)]
        + parts
        + [pltpu.VMEM((n_par, obs // n_par, width), BF16)]
        + [pltpu.VMEM((n_obs, own, width), BF16)] * 2
        + [dma(2)] * 2
        + [dma(n_par)] * 4
        + [dma(n_obs)] * 2,
        compiler_params=params(0),
        name="first_pass",
    )(offsets, probes.reshape(-1, BLK, width), coeffs, jacobian)
    center, lower, upper = pl.pallas_call(
        adjoint_kernel,
        out_shape=[
            jax.ShapeDtypeStruct((own, width), F32),
            jax.ShapeDtypeStruct((HALO, width), BF16),
            jax.ShapeDtypeStruct((HALO, width), BF16),
        ],
        in_specs=[SMEM, VMEM, pl.BlockSpec(memory_space=pl.ANY)],
        out_specs=[VMEM] * 3,
        scratch_shapes=[
            pltpu.VMEM((own + 2 * HALO, width), F32),
            pltpu.VMEM((own // BLK,) + coeffs.shape[1:], BF16),
            dma(1),
        ],
        compiler_params=pltpu.CompilerParams(vmem_limit_bytes=LIMIT),
        name="adjoint_prior",
    )(offsets, adjoint, coeffs)
    block = 64
    full, inverse = pl.pallas_call(
        functools.partial(gram_kernel, n_obs, n_par),
        out_shape=[
            jax.ShapeDtypeStruct((n_obs, own, width), BF16),
            jax.ShapeDtypeStruct((width // block, block, width), F32),
        ],
        in_specs=[VMEM] * 3,
        out_specs=[VMEM] * 2,
        scratch_shapes=[pltpu.VMEM((own, width), F32)]
        + [pltpu.VMEM((HALO, width), BF16)] * 2
        + [pltpu.VMEM((n_obs, n_par, width // count, width), F32)]
        + [pltpu.VMEM((width // block, block, 2 * width), F32)]
        + [dma(2)] * 2
        + [pltpu.SemaphoreType.DMA((2, n_obs))] * 2
        + sum_scratch(n_obs, n_par, width, F32),
        compiler_params=params(1),
        name="gram",
    )(center, lower, upper)
    inverse = inverse.reshape(width, width)
    high_part = inverse.astype(BF16)
    low_part = (inverse - high_part.astype(F32)).astype(BF16)
    sample = full.reshape(rows, width)
    last = (((1,), (1,)), ((), ()))
    basis = (
        lax.dot_general(sample, high_part, last, preferred_element_type=F32)
        + lax.dot_general(sample, low_part, last, preferred_element_type=F32)
    ).astype(BF16)
    image, ritz = pl.pallas_call(
        functools.partial(second_kernel, n_obs, n_par),
        out_shape=[
            jax.ShapeDtypeStruct((rows, width), BF16),
            jax.ShapeDtypeStruct((width, width), F32),
        ],
        in_specs=[SMEM, anywhere, anywhere, anywhere],
        out_specs=[VMEM] * 2,
        scratch_shapes=halos
        + parts
        + [pltpu.VMEM((n_obs, n_par, width // count, width), BF16)]
        + [dma(2)] * 2
        + [dma(n_par)] * 2
        + sum_scratch(n_obs, n_par, width, BF16),
        compiler_params=params(2),
        name="second_pass",
    )(offsets, basis.reshape(-1, BLK, width), coeffs, jacobian)
    return basis, image, ritz


def solution(mesh):
    return jax.shard_map(
        functools.partial(body, mesh.shape["obs"], mesh.shape["par"]),
        mesh=mesh,
        in_specs=(P("obs", "par"), P("par", None), P("par", None, None, None), P("par", None)),
        out_specs=(P("par", None), P("par", None), P()),
        check_vma=False,
    )
```
